256 devices in a mesh: mode: 8 (over z_hi, y), space: 32 (over x, z_lo, core).
Axes of the slice: x: 4, y: 4, z: 8 (z_hi: 2, z_lo: 4; z = z_hi * 4 + z_lo), core: 2. Of those that a mesh axis runs over, the one named last changes fastest.
Arguments:
- energy: float32 [128, 256, 16, 128], P('mode', 'space'), may hold values from -6 to 6
- void: int32 [256, 16, 128], P('space'), may hold values 0 or 1
- spacing_cells: float32 [256, 16, 128], P('space'), may hold values from 2 to 50
- walls: int32 [2, 256, 128], P(None, 'space'), may hold values from 0 to 2
- octant: int32 [128], replicated, may hold values from 0 to 7
- specific_warmth_modes: float32 [128], replicated, may hold values from 0.2 to 2
- second_derivative: float32 [128], replicated, may hold values from 0.5 to 1.5
- umklapp: float32 [128], replicated, may hold values from 0.02 to 1
- isotope: float32 [128], replicated, may hold values from 0.01 to 0.3
- courant: float32 [3, 128], replicated, may hold values from 0.05 to 0.9
Outputs:
- final_energy: float32 [128, 256, 16, 128], P('mode', 'space')
- prior_pseudo_kelvin: float32 [256, 16, 128], P('space')
The draws below stay inside these ranges and needn't reach their ends.
Inputs may be any that keep to these rules, and one draw needn't show every extreme that they name: `walls`: 0 adiabatic wall, 1 cold black wall, 2 hot black wall. `octant`: bit 0, 1 and 2 give a negative direction along the first, second and third dimension.
All inputs are finite; a program needn't handle non-finite values. No bound on the sum of `void` on one device may be relied on, other than what follows from the above.
Results may differ from the reference program's by a relative error of at most 0.0003.
Values sent between devices are 32-bit elements; how exact they have to be, the bound alone decides.
A program may use at most 64 MiB of HBM per device.

```python
import math
import jax
import jax.numpy as jnp
from jax import lax

MODES = 128
NZ = 16
NY = 128
ITERS = 8
STEPS = 1
NX = 256


def with_ends(values, key, least, high):
    shape = values.shape
    place = [jax.random.randint(jax.random.fold_in(key, axis), (), 0, shape[axis]) for axis in range(len(shape))]
    values = values.at[tuple(place)].set(least)
    longest = shape.index(max(shape))
    place[longest] = (place[longest] + 1) % shape[longest]
    return values.at[tuple(place)].set(high)


def block_scale(stream_key, extent, cuts, smallest, top_value):
    factor_of = 1.0
    for axis_at, blocks in cuts:
        heights = jax.random.uniform(jax.random.fold_in(jax.random.fold_in(stream_key, 6), axis_at), (blocks,), jnp.float32, smallest / len(cuts), top_value / len(cuts))
        factor_of = factor_of * jnp.repeat(jnp.exp(heights), extent[axis_at] // blocks).reshape((-1,) + (1,) * (len(extent) - 1 - axis_at))
    return factor_of


def noise(rng, shape, deviation, limit, pieces=(), dtype=jnp.bfloat16):
    gain = block_scale(rng, shape, pieces, -0.22, 0.18) if pieces else 1.0
    drawn = jax.random.normal(rng, shape, jnp.float32) * deviation * gain
    return jnp.minimum(jnp.maximum(drawn, -limit), limit).astype(dtype)


def setup_inputs(seed: int = 0) -> dict:
    key_list = jax.random.split(jax.random.key(seed), 11)
    energy = noise(key_list[0], (MODES, NX, NZ, NY), 1.0, 6.0, ((0, 8), (1, 32)), jnp.float32)
    void = with_ends((jax.random.randint(key_list[1], (NX, NZ, NY), 0, 8) < 1).astype(jnp.int32), jax.random.fold_in(key_list[1], 1), 0, 1)
    spacing_cells = jnp.clip(jnp.exp(math.log(50.0) - 3.218876 * jax.random.uniform(key_list[2], (NX, NZ, NY), jnp.float32) ** block_scale(key_list[2], (NX, NZ, NY), ((0, 32),), -0.2, 0.2)), 2.0, 50.0)
    walls = with_ends(jax.random.randint(key_list[3], (2, NX, NY), 0, 3), jax.random.fold_in(key_list[3], 1), 0, 2).astype(jnp.int32)
    octant = with_ends(jax.random.randint(key_list[4], (MODES,), 0, 8), jax.random.fold_in(key_list[4], 1), 0, 7).astype(jnp.int32)
    specific_warmth_modes = jnp.clip(jnp.exp(jax.random.uniform(key_list[5], (MODES,), jnp.float32, math.log(0.2), math.log(2.0))), 0.2, 2.0)
    second_derivative = jnp.clip(jax.random.uniform(key_list[6], (MODES,), jnp.float32, 0.5, 1.5), 0.5, 1.5)
    umklapp = jnp.clip(jnp.exp(jax.random.uniform(key_list[7], (MODES,), jnp.float32, math.log(0.02), math.log(1.0))), 0.02, 1.0)
    isotope = jnp.clip(jnp.exp(jax.random.uniform(key_list[8], (MODES,), jnp.float32, math.log(0.01), math.log(0.3))), 0.01, 0.3)
    courant = jnp.clip(jnp.exp(jax.random.uniform(key_list[9], (3, MODES), jnp.float32, math.log(0.05), math.log(0.9))), 0.05, 0.9)
    return {"energy": energy, "void": void, "spacing_cells": spacing_cells, "walls": walls, "octant": octant, "specific_warmth_modes": specific_warmth_modes, "second_derivative": second_derivative, "umklapp": umklapp, "isotope": isotope, "courant": courant}


RELAX_WEIGHT = 0.35
HOT_WALL = 1.0

def broadcast_modes(vector):
    return vector[:, None, None, None]

def mode_signs(octant):
    sign_x = 1 - 2 * (octant % 2)
    sign_y = 1 - 2 * (octant // 2 % 2)
    sign_z = 1 - 2 * (octant // 4)
    return (sign_x, sign_y, sign_z)

def transfer_rate(umklapp, isotope, speed, spacing_cells):
    rate = broadcast_modes(umklapp + isotope) + broadcast_modes(speed) / spacing_cells[None]
    return 1.0 - jnp.exp(-rate)

def rest_population(specific_warmth_modes, second_derivative, prior_pseudo_kelvin):
    weighted_quantity = broadcast_modes(second_derivative) * prior_pseudo_kelvin[None]
    return (broadcast_modes(specific_warmth_modes / second_derivative) * jnp.sinh(weighted_quantity), broadcast_modes(specific_warmth_modes) * jnp.cosh(weighted_quantity))

def beam_update(field, near, far, courant_band):
    factor = broadcast_modes(courant_band)
    return field - 0.5 * factor * (3.0 * field - 4.0 * near + far) + 0.5 * factor * factor * (field - 2.0 * near + far)

def beam_rolled(field, courant_band, sign, axis):
    forward = broadcast_modes(sign) > 0
    near = jnp.where(forward, jnp.roll(field, 1, axis), jnp.roll(field, -1, axis))
    far = jnp.where(forward, jnp.roll(field, 2, axis), jnp.roll(field, -2, axis))
    return beam_update(field, near, far, courant_band)

def wall_sweep(field, courant_band, sign, walls, specific_warmth_modes, second_derivative):
    factor = broadcast_modes(courant_band)
    forward = broadcast_modes(sign) > 0
    inflow = broadcast_modes(specific_warmth_modes / second_derivative * jnp.sinh(second_derivative * HOT_WALL))
    bottom = jnp.where(walls[0] == 2, 1.0, 0.0)[None, :, None, :] * inflow
    upper = jnp.where(walls[1] == 2, 1.0, 0.0)[None, :, None, :] * inflow
    from_below = jnp.concatenate([bottom, field[:, :, :-1]], axis=2)
    from_above = jnp.concatenate([field[:, :, 1:], upper], axis=2)
    upstream = jnp.where(forward, from_below, from_above)
    depth = lax.broadcasted_iota(jnp.int32, (1, 1, field.shape[2], 1), 2)
    block_top = (depth == field.shape[2] - 1) & (walls[1] == 0)[None, :, None, :]
    block_bottom = (depth == 0) & (walls[0] == 0)[None, :, None, :]
    blocked = jnp.where(forward, block_top, block_bottom)
    outflow = jnp.where(blocked, 0.0, factor * field)
    return field - outflow + factor * upstream

def reference(energy, void, spacing_cells, walls, octant, specific_warmth_modes, second_derivative, umklapp, isotope, courant):
    fluid = (1 - void).astype(jnp.float32)
    sign_x, sign_y, sign_z = mode_signs(octant)
    speed = jnp.sqrt(lax.optimization_barrier(jnp.sum(courant * courant, axis=0)))
    relax = transfer_rate(umklapp, isotope, speed, spacing_cells)
    iterate_carry = energy * fluid[None]
    prior_pseudo_kelvin = jnp.zeros(spacing_cells.shape, jnp.float32)
    for step in range(STEPS):
        prior_pseudo_kelvin = jnp.zeros(spacing_cells.shape, jnp.float32)
        for sweep in range(ITERS):
            matrix_element, derivative_of_content = rest_population(specific_warmth_modes, second_derivative, prior_pseudo_kelvin)
            balance_mismatch = lax.optimization_barrier(jnp.sum(relax * (matrix_element - iterate_carry), axis=0))
            combined_derivative = lax.optimization_barrier(jnp.sum(relax * derivative_of_content, axis=0))
            prior_pseudo_kelvin = prior_pseudo_kelvin - RELAX_WEIGHT * balance_mismatch / combined_derivative
        matrix_element, derivative_of_content = rest_population(specific_warmth_modes, second_derivative, prior_pseudo_kelvin)
        iterate_carry = iterate_carry + relax * (matrix_element - iterate_carry)
        iterate_carry = beam_rolled(iterate_carry, courant[0], sign_x, 1)
        iterate_carry = wall_sweep(iterate_carry, courant[2], sign_z, walls, specific_warmth_modes, second_derivative)
        iterate_carry = beam_rolled(iterate_carry, courant[1], sign_y, 3)
        iterate_carry = iterate_carry * fluid[None]
    return (iterate_carry, prior_pseudo_kelvin)
```

```python
import functools
import math

import jax
import jax.numpy as jnp
from jax import lax
from jax.experimental import pallas as pl
from jax.experimental.pallas import tpu as pltpu
from jax.sharding import PartitionSpec as P

MESH = pl.DeviceIdType.MESH
F32 = jnp.float32
ITERS = 8
RELAX_WEIGHT = 0.35
TERMS = 23
ROWS = 8
MIDDLE, HALF = 0.26, 0.24
TOP_CURVATURE = 1.5
REACH = 16.0
YS = 4


def place_of_layer(layer):
    return {0: (0, 0), 1: (1, 0), 6: (2, 0), 7: (3, 0), 2: (0, 1), 3: (1, 1), 4: (2, 1), 5: (3, 1)}[layer]


def sinh(x):
    square = x * x
    near_zero = x * (1.0 + square * (1 / 6 + square * (1 / 120 + square * (1 / 5040))))
    return jnp.where(jnp.abs(x) < 0.5, near_zero, 0.5 * (jnp.exp(x) - jnp.exp(-x)))


def splat(value):
    return jnp.full((8, 128), value, F32)


def kernel(
    spaces,
    energy,
    void,
    spacing,
    walls,
    octant,
    warmth,
    curvature,
    umklapp,
    isotope,
    courant,
    out_ref,
    temp_ref,
    e_v,
    void_v,
    space_v,
    walls_v,
    rows_v,
    courant_v,
    octant_s,
    warmth_s,
    curvature_s,
    umklapp_s,
    isotope_s,
    courant_s,
    inverse,
    fluid,
    keep,
    inflow_mask,
    kept,
    relax,
    part,
    part_in,
    total,
    total_in,
    temps,
    temps_in,
    halo_e,
    halo_void,
    halo_space,
    halo_relax,
    table_q,
    table_k,
    table_a,
    lifted,
    local_sem,
    part_send,
    part_recv,
    z_send,
    z_recv,
    t_send,
    t_recv,
    edge_send,
    edge_recv,
    halo_send,
    halo_recv,
):
    bands, layers = energy.shape[0], energy.shape[1]
    me_m, me_s = lax.axis_index("mode"), lax.axis_index("space")
    y, z = lax.rem(me_m, YS), lax.div(me_m, YS)
    first = me_m * bands
    right, left = lax.rem(me_s + 1, spaces), lax.rem(me_s + spaces - 1, spaces)
    peers = [z * YS + lax.rem(y + i, YS) for i in range(1, YS)]
    across = (1 - z) * YS + y

    groups = 4
    per = bands // groups
    loads = [
        pltpu.make_async_copy(src, dst, local_sem.at[i])
        for i, (src, dst) in enumerate(
            [
                (spacing, space_v),
                (void, void_v),
                (umklapp, umklapp_s),
                (isotope, isotope_s),
                (courant, courant_s),
            ]
            + [(energy.at[pl.ds(g * per, per)], e_v.at[pl.ds(g * per, per)]) for g in range(groups)]
            + [
                (warmth, warmth_s),
                (curvature, curvature_s),
                (octant, octant_s),
                (warmth, rows_v.at[0]),
                (curvature, rows_v.at[1]),
                (umklapp, rows_v.at[2]),
                (isotope, rows_v.at[3]),
                (courant, courant_v),
                (walls, walls_v),
            ]
        )
    ]
    for copy in loads:
        copy.start()

    barrier = pltpu.get_barrier_semaphore()

    def tell(mode, space):
        pl.semaphore_signal(barrier, inc=1, device_id={"mode": mode, "space": space}, device_id_type=MESH)

    for peer in peers:
        tell(peer, me_s)
    tell(across, me_s)
    tell(me_m, right)
    tell(me_m, left)
    tell(z * YS + 0, right)
    tell(z * YS + 1, right)
    tell(z * YS + 2, left)
    tell(z * YS + 3, left)

    for copy in loads[:5]:
        copy.wait()
    inverse[...] = 1.0 / space_v[...]
    fluid[...] = (1 - void_v[...]).astype(F32)

    def rates(band):
        c0, c1, c2 = (splat(courant_s[i, band]) for i in range(3))
        speed = jnp.sqrt(c0 * c0 + c1 * c1 + c2 * c2)
        return splat(umklapp_s[band]) + splat(isotope_s[band]), speed

    shares = [jnp.zeros((16, 128), F32) for _ in range(layers)]
    for g in range(groups):
        loads[5 + g].wait()

        def share(i, sums, g=g):
            b = g * per + i
            base, speed = rates(first + b)
            base, speed = jnp.tile(base, (2, 1)), jnp.tile(speed, (2, 1))
            new = []
            for layer in range(layers):
                left_over = jnp.exp(-(base + speed * inverse[layer]))
                state = e_v[b, layer] * fluid[layer]
                held = left_over * state
                kept[b, layer + 2] = held
                relax[b, layer] = 1.0 - left_over
                new.append(sums[layer] + (state - held))
            return new

        shares = lax.fori_loop(0, per, share, shares)
    for layer in range(layers):
        part[place_of_layer(layer)] = shares[layer]

    pl.semaphore_wait(barrier, 10)

    part_copies = [
        pltpu.make_async_remote_copy(
            src_ref=part.at[lax.rem(y + i, YS)],
            dst_ref=part_in.at[3 - i],
            send_sem=part_send.at[i - 1],
            recv_sem=part_recv.at[3 - i],
            device_id={"mode": peers[i - 1]},
            device_id_type=MESH,
        )
        for i in range(1, YS)
    ]
    for copy in part_copies:
        copy.start()

    halo_copies = []
    for side, (target, start) in enumerate(((right, layers - 2), (left, 0))):
        for i, (src, dst) in enumerate(
            (
                (energy.at[:, pl.ds(start, 2)], halo_e.at[side]),
                (spacing.at[pl.ds(start, 2)], halo_space.at[side]),
                (void.at[pl.ds(start, 2)], halo_void.at[side]),
            )
        ):
            halo_copies.append(
                pltpu.make_async_remote_copy(
                    src_ref=src,
                    dst_ref=dst,
                    send_sem=halo_send.at[side * 3 + i],
                    recv_sem=halo_recv.at[side * 3 + i],
                    device_id={"space": target},
                    device_id_type=MESH,
                )
            )
    for copy in halo_copies:
        copy.start()

    for copy in loads[5 + groups :]:
        copy.wait()
    warm_row, curve_row = rows_v[0:1, :], rows_v[1:2, :]
    c_rows = courant_v[...]
    speed_row = jnp.sqrt(jnp.sum(c_rows * c_rows, axis=0, keepdims=True))
    weight = jnp.exp(-(rows_v[2:3, :] + rows_v[3:4, :] + MIDDLE * speed_row))
    slant = HALF * speed_row
    power = jnp.ones_like(slant)
    powers = []
    for j in range(ROWS + 1):
        powers.append(power * (1.0 / math.factorial(j)))
        power = power * (-slant)
    fold = {0: -1 / 128, 2: 0.25, 4: -1.25, 6: 2.0}
    for j in range(ROWS):
        row = powers[j] + fold[j] * powers[ROWS] if j in fold else powers[j]
        row = -weight * row
        table_q[j : j + 1, :] = 1.0 + row if j == 0 else row
    q = table_q[...]
    ratio = curve_row * (1.0 / TOP_CURVATURE)
    ratio = jnp.broadcast_to(ratio * ratio, (8, 128))
    grown = jnp.broadcast_to(warm_row, (8, 128))
    for k in range(TERMS):
        factor = REACH ** (2 * k) / math.factorial(2 * k + 1)
        moment = jnp.sum(q * grown, axis=1, keepdims=True) * factor
        table_k[k] = jnp.broadcast_to(moment, (8, 128))
        grown = grown * ratio
    edge, inner = y + 4 * lax.div(y, 2), y + 2
    v = jnp.concatenate([inverse[edge], inverse[inner]], axis=0)
    v = (v - MIDDLE) * (1.0 / HALF)
    for k in range(TERMS):
        value = jnp.broadcast_to(table_k[k, ROWS - 1 : ROWS, :], v.shape)
        for j in range(ROWS - 2, -1, -1):
            value = value * v + table_k[k, j : j + 1, :]
        table_a[k] = value

    depth = lax.broadcasted_iota(jnp.int32, (16, 128), 0)
    for layer in range(layers):
        bottom, upper = walls_v[0, layer : layer + 1, :], walls_v[1, layer : layer + 1, :]
        inflow_mask[0, layer : layer + 1, :] = jnp.where(bottom == 2, 1.0, 0.0)
        inflow_mask[1, layer : layer + 1, :] = jnp.where(upper == 2, 1.0, 0.0)
        keep[0, layer] = jnp.where((depth == 15) & (upper == 0), 0.0, 1.0)
        keep[1, layer] = jnp.where((depth == 0) & (bottom == 0), 0.0, 1.0)

    for copy in part_copies:
        copy.wait_recv()
    total[...] = (part[y] + part_in[0]) + (part_in[1] + part_in[2])
    z_copy = pltpu.make_async_remote_copy(
        src_ref=total,
        dst_ref=total_in,
        send_sem=z_send,
        recv_sem=z_recv,
        device_id={"mode": across},
        device_id_type=MESH,
    )
    z_copy.start()
    z_copy.wait_recv()
    goal = (total[...] + total_in[...]).reshape(32, 128)

    def newton(_, temp):
        scaled = temp * (TOP_CURVATURE / REACH)
        square = scaled * scaled
        value = table_a[TERMS - 1]
        slope = jnp.zeros_like(value)
        for k in range(TERMS - 2, -1, -1):
            slope = slope * square + value
            value = value * square + table_a[k]
        slope = value + 2.0 * square * slope
        return temp - RELAX_WEIGHT * (temp * value - goal) / slope

    temp = RELAX_WEIGHT * goal / table_a[0]
    temp = lax.fori_loop(1, ITERS, newton, temp)
    temps[y] = temp.reshape(2, 16, 128)

    t_copies = [
        pltpu.make_async_remote_copy(
            src_ref=temps.at[y],
            dst_ref=temps.at[y],
            send_sem=t_send.at[i - 1],
            recv_sem=t_recv.at[3 - i],
            device_id={"mode": peers[i - 1]},
            device_id_type=MESH,
        )
        for i in range(1, YS)
    ]
    beside = lax.rem(me_s + spaces - 1 + 2 * lax.div(y, 2), spaces)
    slot = lax.rem(y + 2, YS)
    edge_copies = [
        pltpu.make_async_remote_copy(
            src_ref=temps.at[y, 0],
            dst_ref=temps_in.at[slot],
            send_sem=edge_send.at[i],
            recv_sem=edge_recv.at[slot],
            device_id={"mode": z * YS + i, "space": beside},
            device_id_type=MESH,
        )
        for i in range(YS)
    ]
    for copy in t_copies + edge_copies:
        copy.start()

    for copy in halo_copies:
        copy.wait_recv()

    def halo_share(b, _):
        base, speed = rates(first + b)
        base, speed = jnp.tile(base, (2, 1)), jnp.tile(speed, (2, 1))
        for side in range(2):
            for i in range(2):
                left_over = jnp.exp(-(base + speed / halo_space[side, i]))
                state = halo_e[side, b, i] * (1 - halo_void[side, i]).astype(F32)
                kept[b, side * (layers + 2) + i] = left_over * state
                halo_relax[b, side * 2 + i] = 1.0 - left_over
        return _

    lax.fori_loop(0, bands, halo_share, 0)

    for copy in t_copies:
        copy.wait_recv()
    for layer in range(layers):
        temp_ref[layer] = temps[place_of_layer(layer)]

    def equilibrium(band):
        bend = splat(curvature_s[band])
        scale = splat(warmth_s[band]) / bend
        return jnp.tile(bend, (2, 1)), jnp.tile(scale, (2, 1))

    def sweep(b, which, bend, scale):
        band = first + b
        kind = octant_s[band]
        back_x, back_y, back_z = kind & 1, (kind >> 1) & 1, (kind >> 2) & 1
        step_x = 1 - 2 * back_x
        cx, cy, cz = (jnp.full((16, 128), courant_s[i, band], F32) for i in range(3))
        x_near, x_far = cx * (2.0 - cx), cx * (0.5 * cx - 0.5)
        x_own = 1.0 - x_near - x_far
        y_near, y_far = cy * (2.0 - cy), cy * (0.5 * cy - 0.5)
        y_own = 1.0 - y_near - y_far
        inflow = (scale * sinh(bend))[0:1, :]
        for layer in which:
            own = kept[b, layer + 2]
            near = kept[b, layer + 2 - step_x]
            far = kept[b, layer + 2 - 2 * step_x]
            lifted[layer, 8:24, :] = x_own * own + x_near * near + x_far * far
            lifted[layer, 7:8, :] = inflow * inflow_mask[0, layer : layer + 1, :]
            lifted[layer, 24:25, :] = inflow * inflow_mask[1, layer : layer + 1, :]
        turn_near, turn_far = 1 + 126 * back_y, 2 + 124 * back_y
        for layer in which:
            field = lifted[layer, 8:24, :]
            upstream = lifted[layer, pl.ds(7 + 2 * back_z, 16), :]
            field = field - cz * keep[back_z, layer] * field + cz * upstream
            near = pltpu.roll(field, turn_near, 1)
            far = pltpu.roll(field, turn_far, 1)
            out_ref[b, layer] = (y_own * field + y_near * near + y_far * far) * fluid[layer]

    def inner_layers(b, _):
        bend, scale = equilibrium(first + b)
        for layer in range(layers):
            level = scale * sinh(bend * temps[place_of_layer(layer)])
            kept[b, layer + 2] = kept[b, layer + 2] + relax[b, layer] * level
        sweep(b, range(2, layers - 2), bend, scale)
        return _

    lax.fori_loop(0, bands, inner_layers, 0)

    for i in range(YS):
        pltpu.make_async_remote_copy(
            src_ref=temps.at[y, 0],
            dst_ref=temps_in.at[i],
            send_sem=edge_send.at[i],
            recv_sem=edge_recv.at[i],
            device_id={"mode": z * YS + i, "space": beside},
            device_id_type=MESH,
        ).wait_recv()

    def edge_layers(b, _):
        bend, scale = equilibrium(first + b)
        for i in range(4):
            at = i if i < 2 else layers + i
            level = scale * sinh(bend * temps_in[i])
            kept[b, at] = kept[b, at] + halo_relax[b, i] * level
        sweep(b, (0, 1, layers - 2, layers - 1), bend, scale)
        return _

    lax.fori_loop(0, bands, edge_layers, 0)

    for copy in part_copies + [z_copy] + t_copies + edge_copies + halo_copies:
        copy.wait_send()


def local(spaces, energy, void, spacing, walls, octant, warmth, curvature, umklapp, isotope, courant):
    bands, layers, deep, wide = energy.shape
    vmem = lambda *shape: pltpu.VMEM(shape, F32)
    dma = lambda *shape: pltpu.SemaphoreType.DMA(shape)
    return pl.pallas_call(
        functools.partial(kernel, spaces),
        out_shape=(
            jax.ShapeDtypeStruct(energy.shape, F32),
            jax.ShapeDtypeStruct(spacing.shape, F32),
        ),
        in_specs=[pl.BlockSpec(memory_space=pl.ANY)] * 10,
        out_specs=(pl.BlockSpec(memory_space=pltpu.VMEM),) * 2,
        scratch_shapes=[
            vmem(bands, layers, deep, wide),
            pltpu.VMEM((layers, deep, wide), jnp.int32),
            vmem(layers, deep, wide),
            pltpu.VMEM((2, layers, wide), jnp.int32),
            vmem(8, wide),
            vmem(3, wide),
            pltpu.SMEM((128,), jnp.int32),
            pltpu.SMEM((128,), F32),
            pltpu.SMEM((128,), F32),
            pltpu.SMEM((128,), F32),
            pltpu.SMEM((128,), F32),
            pltpu.SMEM((3, 128), F32),
            vmem(layers, deep, wide),
            vmem(layers, deep, wide),
            vmem(2, layers, deep, wide),
            vmem(2, layers, wide),
            vmem(bands, layers + 4, deep, wide),
            vmem(bands, layers, deep, wide),
            vmem(YS, 2, deep, wide),
            vmem(3, 2, deep, wide),
            vmem(2, deep, wide),
            vmem(2, deep, wide),
            vmem(YS, 2, deep, wide),
            vmem(YS, deep, wide),
            vmem(2, bands, 2, deep, wide),
            pltpu.VMEM((2, 2, deep, wide), jnp.int32),
            vmem(2, 2, deep, wide),
            vmem(bands, 4, deep, wide),
            vmem(8, wide),
            vmem(TERMS, 8, wide),
            vmem(TERMS, 32, wide),
            vmem(layers, 32, wide),
            dma(24),
            dma(3),
            dma(3),
            dma(),
            dma(),
            dma(3),
            dma(3),
            dma(4),
            dma(4),
            dma(6),
            dma(6),
        ],
        compiler_params=pltpu.CompilerParams(collective_id=0, has_side_effects=True),
        name="transport",
    )(energy, void, spacing, walls, octant, warmth, curvature, umklapp, isotope, courant)


def solution(mesh):
    in_specs = (
        P("mode", "space", None, None),
        P("space", None, None),
        P("space", None, None),
        P(None, "space", None),
        P(),
        P(),
        P(),
        P(),
        P(),
        P(),
    )
    out_specs = (P("mode", "space", None, None), P("space", None, None))
    return jax.shard_map(
        functools.partial(local, mesh.shape["space"]),
        mesh=mesh,
        in_specs=in_specs,
        out_specs=out_specs,
        check_vma=False,
    )
```
